32 devices in a mesh: gx: 16 (over z, y, x), gy: 2 (over core).
Axes of the slice: x: 2, y: 2, z: 4, core: 2. Of those that a mesh axis runs over, the one named last changes fastest.
Arguments:
- moisture_ratio: float32 [2, 128, 256], P(None, 'gx', 'gy'), may hold values from 11 to 14
- kelvin_warmth: float32 [2, 128, 256], P(None, 'gx', 'gy'), may hold values from 286 to 292
- droplet_size_micron: float32 [8, 2, 128, 256], P(None, None, 'gx', 'gy'), may hold values from 0.5 to 25
- weighting_factor: float32 [8, 2, 128, 256], P(None, None, 'gx', 'gy'), may hold values from 0.1 to 2
- dry_nucleus_size: float32 [8, 2, 128, 256], P(None, None, 'gx', 'gy'), may hold values from 0.02 to 0.3
- fractional_offset_east: float32 [8, 2, 128, 256], P(None, None, 'gx', 'gy'), may hold values from 0 to 1
- fractional_offset_north: float32 [8, 2, 128, 256], P(None, None, 'gx', 'gy'), may hold values from 0 to 1
- encounter_permutation: int32 [8, 2, 128, 256], P(None, None, 'gx', 'gy'), may hold values from 0 to 7, as said below
- departing_eastwest_lists: int32 [16, 2, 2048], P('gx', None, 'gy'), may hold values from -1 to 16383, as said below
- departing_northsouth_lists: int32 [16, 2, 96], P('gx', None, 'gy'), may hold values from -1 to 16383, as said below
- departing_diagonal_lists: int32 [16, 4, 16], P('gx', None, 'gy'), may hold values from -1 to 16383, as said below
Outputs:
- resulting_moisture_ratio: float32 [2, 128, 256], P(None, 'gx', 'gy')
- resulting_kelvin_value: float32 [2, 128, 256], P(None, 'gx', 'gy')
- resulting_droplet_size: float32 [8, 2, 128, 256], P(None, None, 'gx', 'gy')
- resulting_weighting_factor: float32 [8, 2, 128, 256], P(None, None, 'gx', 'gy')
- arrival_particle_records: float32 [5, 16, 4352], P(None, 'gx', 'gy')
- arrival_box_index: int32 [16, 4352], P('gx', 'gy')
The draws below stay inside these ranges and needn't reach their ends.
Inputs may be any that keep to these rules, and one draw needn't show every extreme that they name: `encounter_permutation`: along the first dimension, the 8 entries of each cell are a permutation of 0 to 7. `departing_eastwest_lists`: each list holds live slot numbers of its own device first and -1 after them, at most 1024 live, and some list of some device is full. Row 0 names only droplets of cells with i = 7, row 1 only i = 0, both only 0 < j < 127. No slot is named twice among all lists of a device. `departing_northsouth_lists`: each list holds live slot numbers of its own device first and -1 after them, at most 48 live, and some list of some device is full. Row 0 names only droplets of cells with j = 127, row 1 only j = 0, both only 0 < i < 7. `departing_diagonal_lists`: each list holds live slot numbers of its own device first and -1 after them, at most 8 live, and some list of some device is full. Row r names only droplets of the corner cell that its move points to: i = 7 for rows 0 and 1, i = 0 for rows 2 and 3, j = 127 for rows 0 and 2, j = 0 for rows 1 and 3.
All inputs are finite; a program needn't handle non-finite values.
Results may differ from the reference program's by a relative error of at most 0.0003.
Values sent between devices are 32-bit elements; how exact they have to be, the bound alone decides.
A program may use at most 64 MiB of HBM per device.

```python
import math
import jax
import jax.numpy as jnp
from jax import lax

NUMBER_OF_TIERS = 2
SD = 8
NEWTON = 4
CX = 8
CY = 128
GRID_WIDTH_EAST = 128
GRID_WIDTH_NORTH = 256
DROPS = 16384
KX = 1024
KY = 48
KC = 8
NARR = 2176
N_GX = 16
N_GY = 2


def draw_lists(key, list_rows, list_length, eligible, slot_of):
    grid_x = GRID_WIDTH_EAST // CX
    grid_y = GRID_WIDTH_NORTH // CY
    total_lists = grid_x * list_rows * grid_y
    keys = jax.random.split(key, total_lists)
    chosen = jax.vmap(lambda single: jax.random.permutation(single, eligible)[:list_length])(keys)
    chosen = chosen.reshape(grid_x, list_rows, grid_y, list_length).astype(jnp.int32)
    direction = lax.broadcasted_iota(jnp.int32, chosen.shape, 1)
    slots = slot_of(chosen, direction).astype(jnp.int32)
    live_count = jax.random.randint(jax.random.fold_in(key, 1), (grid_x, list_rows, grid_y, 1), list_length // 4, list_length + 1)
    fullest = jax.random.randint(jax.random.fold_in(key, 2), (), 0, total_lists)
    list_id = (lax.broadcasted_iota(jnp.int32, live_count.shape, 0) * list_rows + lax.broadcasted_iota(jnp.int32, live_count.shape, 1)) * grid_y + lax.broadcasted_iota(jnp.int32, live_count.shape, 2)
    live_count = jnp.where(list_id == fullest, list_length, live_count)
    position = lax.broadcasted_iota(jnp.int32, chosen.shape, 3)
    result = jnp.where(position < live_count, slots, -1)
    return result.reshape(grid_x, list_rows, grid_y * list_length).astype(jnp.int32)


def draw_departing_eastwest_lists(key, part):
    inner_width = CY - 2

    def slot_of(chosen, direction):
        stack_level = chosen // inner_width
        index_y = chosen % inner_width + 1
        index_x = jnp.where(direction == 0, CX - 1, 0)
        return (stack_level * CX + index_x) * CY + index_y
    return draw_lists(jax.random.fold_in(key, 11), 2, KX, SD * NUMBER_OF_TIERS * inner_width, slot_of)


def draw_departing_northsouth_lists(key, part):
    inner_width = CX - 2

    def slot_of(chosen, direction):
        stack_level = chosen // inner_width
        index_x = chosen % inner_width + 1
        index_y = jnp.where(direction == 0, CY - 1, 0)
        return (stack_level * CX + index_x) * CY + index_y
    return draw_lists(jax.random.fold_in(key, 12), 2, KY, SD * NUMBER_OF_TIERS * inner_width, slot_of)


def draw_departing_diagonal_lists(key, part):

    def slot_of(chosen, direction):
        index_x = jnp.where(direction < 2, CX - 1, 0)
        index_y = jnp.where(direction % 2 == 0, CY - 1, 0)
        return (chosen * CX + index_x) * CY + index_y
    return draw_lists(jax.random.fold_in(key, 13), 4, KC, SD * NUMBER_OF_TIERS, slot_of)


def draw_encounter_permutation(key, part):
    shape_all = (SD, NUMBER_OF_TIERS, GRID_WIDTH_EAST, GRID_WIDTH_NORTH)
    scores = jax.random.randint(jax.random.fold_in(key, 14), shape_all, 0, 1 << 20) * SD + lax.broadcasted_iota(jnp.int32, shape_all, 0)
    return jnp.argsort(scores, axis=0).astype(jnp.int32)


def block_scale(own_key, extent, cuts, smallest, largest):
    level = 1.0
    for axis_at, blocks in cuts:
        steps = jax.random.uniform(jax.random.fold_in(jax.random.fold_in(own_key, 6), axis_at), (blocks,), jnp.float32, smallest / len(cuts), largest / len(cuts))
        level = level * jnp.repeat(jnp.exp(steps), extent[axis_at] // blocks).reshape((-1,) + (1,) * (len(extent) - 1 - axis_at))
    return level


def setup_inputs(seed: int = 0) -> dict:
    seeds = jax.random.split(jax.random.key(seed), 12)
    return {
        "moisture_ratio": jnp.clip(11.0 + 3.0 * jax.random.uniform(seeds[0], (NUMBER_OF_TIERS, GRID_WIDTH_EAST, GRID_WIDTH_NORTH), jnp.float32) ** block_scale(seeds[0], (NUMBER_OF_TIERS, GRID_WIDTH_EAST, GRID_WIDTH_NORTH), ((1, 16), (2, 2)), -0.2, 0.2), 11.0, 14.0),
        "kelvin_warmth": jnp.clip(286.0 + 6.0 * jax.random.uniform(seeds[1], (NUMBER_OF_TIERS, GRID_WIDTH_EAST, GRID_WIDTH_NORTH), jnp.float32) ** block_scale(seeds[1], (NUMBER_OF_TIERS, GRID_WIDTH_EAST, GRID_WIDTH_NORTH), ((1, 16), (2, 2)), -0.2, 0.2), 286.0, 292.0),
        "droplet_size_micron": jnp.clip(jnp.exp(math.log(25.0) - 3.912023 * jax.random.uniform(seeds[2], (SD, NUMBER_OF_TIERS, GRID_WIDTH_EAST, GRID_WIDTH_NORTH), jnp.float32) ** block_scale(seeds[2], (SD, NUMBER_OF_TIERS, GRID_WIDTH_EAST, GRID_WIDTH_NORTH), ((2, 16), (3, 2)), -0.2, 0.2)), 0.5, 25.0),
        "weighting_factor": jnp.clip(jnp.exp(math.log(2.0) - 2.9957323 * jax.random.uniform(seeds[3], (SD, NUMBER_OF_TIERS, GRID_WIDTH_EAST, GRID_WIDTH_NORTH), jnp.float32) ** block_scale(seeds[3], (SD, NUMBER_OF_TIERS, GRID_WIDTH_EAST, GRID_WIDTH_NORTH), ((2, 16), (3, 2)), -0.2, 0.2)), 0.1, 2.0),
        "dry_nucleus_size": jnp.clip(jnp.exp(math.log(0.3) - 2.7080503 * jax.random.uniform(seeds[4], (SD, NUMBER_OF_TIERS, GRID_WIDTH_EAST, GRID_WIDTH_NORTH), jnp.float32) ** block_scale(seeds[4], (SD, NUMBER_OF_TIERS, GRID_WIDTH_EAST, GRID_WIDTH_NORTH), ((2, 16), (3, 2)), -0.2, 0.2)), 0.02, 0.3),
        "fractional_offset_east": jnp.clip(1.0 * jax.random.uniform(seeds[5], (SD, NUMBER_OF_TIERS, GRID_WIDTH_EAST, GRID_WIDTH_NORTH), jnp.float32) ** block_scale(seeds[5], (SD, NUMBER_OF_TIERS, GRID_WIDTH_EAST, GRID_WIDTH_NORTH), ((2, 16), (3, 2)), -0.2, 0.2), 0.0, 1.0),
        "fractional_offset_north": jnp.clip(1.0 * jax.random.uniform(seeds[6], (SD, NUMBER_OF_TIERS, GRID_WIDTH_EAST, GRID_WIDTH_NORTH), jnp.float32) ** block_scale(seeds[6], (SD, NUMBER_OF_TIERS, GRID_WIDTH_EAST, GRID_WIDTH_NORTH), ((2, 16), (3, 2)), -0.2, 0.2), 0.0, 1.0),
        "encounter_permutation": draw_encounter_permutation(jax.random.fold_in(seeds[11], 71), 0),
        "departing_eastwest_lists": draw_departing_eastwest_lists(jax.random.fold_in(seeds[11], 71), 0),
        "departing_northsouth_lists": draw_departing_northsouth_lists(jax.random.fold_in(seeds[11], 71), 0),
        "departing_diagonal_lists": draw_departing_diagonal_lists(jax.random.fold_in(seeds[11], 71), 0),
    }


MIX_HORIZONTAL = 0.2
MIX_VERTICAL = 0.05
EXCESS_FACTOR = 4.2222
CURVATURE = 0.0012
KAPPA_SOLUTE = 0.6
GROWTH_STEP = 200.0
COLLIDE_RATE = 4e-07
VAPOUR_PER_SOURCE = 0.001
WARMING_FACTOR = 0.00249

def moisture_excess(moisture_ratio, kelvin_warmth):
    maximum_list_length = EXCESS_FACTOR * jnp.exp(17.27 * (kelvin_warmth - 273.15) / (kelvin_warmth - 35.86))
    return moisture_ratio / maximum_list_length - 1.0

def kernel_weights(offset):
    return (jnp.maximum(0.5 - offset, 0.0), 1.0 - jnp.abs(offset - 0.5), jnp.maximum(offset - 0.5, 0.0))

def vertical_mix(centre, level_axis):
    levels = centre.shape[level_axis]
    above = jnp.concatenate([lax.slice_in_dim(centre, 1, levels, axis=level_axis), lax.slice_in_dim(centre, levels - 1, levels, axis=level_axis)], level_axis)
    below = jnp.concatenate([lax.slice_in_dim(centre, 0, 1, axis=level_axis), lax.slice_in_dim(centre, 0, levels - 1, axis=level_axis)], level_axis)
    return above + below - 2.0 * centre

def domain_wide_stirring(field):
    horizontal = jnp.roll(field, 1, 1) + jnp.roll(field, -1, 1) + jnp.roll(field, 1, 2) + jnp.roll(field, -1, 2) - 4.0 * field
    return field + MIX_HORIZONTAL * horizontal + MIX_VERTICAL * vertical_mix(field, 0)

def grow_droplets(droplet_size_micron, dry_nucleus_size, forcing):
    initial = droplet_size_micron * droplet_size_micron
    solute = KAPPA_SOLUTE * dry_nucleus_size * dry_nucleus_size * dry_nucleus_size
    lowest = dry_nucleus_size * dry_nucleus_size
    wetted = initial
    for sweep in range(NEWTON):
        root_wet = jnp.sqrt(wetted)
        inverse = 1.0 / (wetted * root_wet)
        residue = wetted - initial - GROWTH_STEP * (forcing + solute * inverse)
        slope_value = 1.0 + 1.5 * GROWTH_STEP * solute * inverse / wetted
        wetted = jnp.maximum(wetted - residue / slope_value, lowest)
    return wetted

def coalesce(grown_radius, weighting_factor, encounter_permutation):
    ordered_radius = jnp.take_along_axis(grown_radius, encounter_permutation, axis=0)
    ordered_mult = jnp.take_along_axis(weighting_factor, encounter_permutation, axis=0)
    first_radius = ordered_radius[0::2]
    second_radius = ordered_radius[1::2]
    first_mult = ordered_mult[0::2]
    second_mult = ordered_mult[1::2]
    first_big = first_mult >= second_mult
    high_radius = jnp.where(first_big, first_radius, second_radius)
    low_radius = jnp.where(first_big, second_radius, first_radius)
    high_mult = jnp.where(first_big, first_mult, second_mult)
    low_mult = jnp.where(first_big, second_mult, first_mult)
    radius_sum = first_radius + second_radius
    kernel = COLLIDE_RATE * high_mult * radius_sum * radius_sum * jnp.abs(first_radius * first_radius - second_radius * second_radius)
    chance = 1.0 - jnp.exp(-kernel)
    merged_radius = jnp.cbrt(low_radius * low_radius * low_radius + chance * high_radius * high_radius * high_radius)
    reduced_mult = high_mult - chance * low_mult
    new_first_radius = jnp.where(first_big, high_radius, merged_radius)
    new_second_radius = jnp.where(first_big, merged_radius, high_radius)
    new_first_mult = jnp.where(first_big, reduced_mult, low_mult)
    new_second_mult = jnp.where(first_big, low_mult, reduced_mult)
    paired_radius = jnp.stack([new_first_radius, new_second_radius], 1).reshape(grown_radius.shape)
    paired_mult = jnp.stack([new_first_mult, new_second_mult], 1).reshape(grown_radius.shape)
    positions = lax.broadcasted_iota(jnp.int32, encounter_permutation.shape, 0)
    ranks = []
    for target in range(encounter_permutation.shape[0]):
        ranks.append(lax.optimization_barrier(jnp.sum(jnp.where(encounter_permutation == target, positions, 0), axis=0)))
    slot_rank = jnp.stack(ranks, 0).astype(jnp.int32)
    return (jnp.take_along_axis(paired_radius, slot_rank, axis=0), jnp.take_along_axis(paired_mult, slot_rank, axis=0))

def to_blocks(values):
    return values.reshape(SD, NUMBER_OF_TIERS, N_GX, CX, N_GY, CY).transpose(2, 4, 0, 1, 3, 5).reshape(N_GX, N_GY, DROPS)

def from_blocks(values):
    return values.reshape(N_GX, N_GY, SD, NUMBER_OF_TIERS, CX, CY).transpose(2, 3, 0, 4, 1, 5).reshape(SD, NUMBER_OF_TIERS, N_GX * CX, N_GY * CY)

def list_blocks(lists, list_rows, list_length):
    return lists.reshape(N_GX, list_rows, N_GY, list_length).transpose(0, 2, 1, 3)

def make_records(attr_table, lists, directions):
    list_rows = lists.shape[2]
    list_length = lists.shape[3]
    is_live = lists >= 0
    safe_slot = jnp.where(is_live, lists, 0).astype(jnp.int32)
    take_index = jnp.broadcast_to(safe_slot.reshape(N_GX, N_GY, 1, list_rows * list_length), (N_GX, N_GY, 5, list_rows * list_length))
    picked = jnp.take_along_axis(attr_table, take_index, axis=3)
    picked = picked.reshape(N_GX, N_GY, 5, list_rows, list_length).transpose(0, 1, 3, 2, 4)
    picked = jnp.where(is_live[:, :, :, None, :], picked, 0.0)
    cell_index = safe_slot % (NUMBER_OF_TIERS * CX * CY)
    level_index = cell_index // (CX * CY)
    index_x = cell_index // CY % CX
    index_y = cell_index % CY
    move_x = jnp.array([entry[0] for entry in directions], jnp.int32).reshape(1, 1, list_rows, 1)
    move_y = jnp.array([entry[1] for entry in directions], jnp.int32).reshape(1, 1, list_rows, 1)
    target = (level_index * CX + (index_x + move_x) % CX) * CY + (index_y + move_y) % CY
    target = jnp.where(is_live, target, -1).astype(attr_table.dtype)
    return jnp.concatenate([picked, target[:, :, :, None, :]], 3)

def reference(moisture_ratio, kelvin_warmth, droplet_size_micron, weighting_factor, dry_nucleus_size, fractional_offset_east, fractional_offset_north, encounter_permutation, departing_eastwest_lists, departing_northsouth_lists, departing_diagonal_lists):
    averaged_moisture_ratio = domain_wide_stirring(moisture_ratio)
    averaged_warmth_kelvin = domain_wide_stirring(kelvin_warmth)
    moisture_fraction = moisture_excess(averaged_moisture_ratio, averaged_warmth_kelvin)
    weight_x = kernel_weights(fractional_offset_east)
    weight_y = kernel_weights(fractional_offset_north)
    forcing = jnp.zeros_like(droplet_size_micron)
    for shift_x in range(3):
        for shift_y in range(3):
            shifted = jnp.roll(moisture_fraction, (1 - shift_x, 1 - shift_y), (1, 2))
            forcing = forcing + weight_x[shift_x] * weight_y[shift_y] * shifted[None]
    forcing = forcing - CURVATURE / droplet_size_micron
    wetted = grow_droplets(droplet_size_micron, dry_nucleus_size, forcing)
    condensed = weighting_factor * (wetted * jnp.sqrt(wetted) - droplet_size_micron * droplet_size_micron * droplet_size_micron)
    deposition_rate_term = jnp.zeros_like(moisture_ratio)
    for shift_x in range(3):
        for shift_y in range(3):
            deposit = lax.optimization_barrier(jnp.sum(weight_x[shift_x] * weight_y[shift_y] * condensed, axis=0))
            deposition_rate_term = deposition_rate_term + jnp.roll(deposit, (shift_x - 1, shift_y - 1), (1, 2))
    resulting_moisture_ratio = averaged_moisture_ratio - VAPOUR_PER_SOURCE * deposition_rate_term
    resulting_kelvin_value = averaged_warmth_kelvin + WARMING_FACTOR * deposition_rate_term
    grown_radius = jnp.sqrt(wetted)
    resulting_droplet_size, coalesced = coalesce(grown_radius, weighting_factor, encounter_permutation)
    lists_x = list_blocks(departing_eastwest_lists, 2, KX)
    lists_y = list_blocks(departing_northsouth_lists, 2, KY)
    lists_corner = list_blocks(departing_diagonal_lists, 4, KC)
    all_lists = jnp.concatenate([lists_x.reshape(N_GX, N_GY, -1), lists_y.reshape(N_GX, N_GY, -1), lists_corner.reshape(N_GX, N_GY, -1)], 2)
    grid_first = lax.broadcasted_iota(jnp.int32, all_lists.shape, 0)
    grid_second = lax.broadcasted_iota(jnp.int32, all_lists.shape, 1)
    whole_count = N_GX * N_GY * DROPS
    flat_slot = jnp.where(all_lists >= 0, (grid_first * N_GY + grid_second) * DROPS + all_lists, whole_count)
    departed = jnp.zeros((whole_count,), droplet_size_micron.dtype).at[flat_slot.reshape(-1)].set(1.0, mode='drop')
    departed = from_blocks(departed.reshape(N_GX, N_GY, DROPS))
    resulting_weighting_factor = jnp.where(departed > 0.0, 0.0, coalesced)
    attr_table = jnp.stack([to_blocks(resulting_droplet_size), to_blocks(coalesced), to_blocks(dry_nucleus_size), to_blocks(fractional_offset_east), to_blocks(fractional_offset_north)], 2)
    records_x = make_records(attr_table, lists_x, ((1, 0), (-1, 0)))
    records_y = make_records(attr_table, lists_y, ((0, 1), (0, -1)))
    records_corner = make_records(attr_table, lists_corner, ((1, 1), (1, -1), (-1, 1), (-1, -1)))
    from_west = jnp.roll(records_x[:, :, 0], 1, 0)
    from_east = jnp.roll(records_x[:, :, 1], -1, 0)
    from_south = jnp.roll(records_y[:, :, 0], 1, 1)
    from_north = jnp.roll(records_y[:, :, 1], -1, 1)
    south_west = jnp.roll(records_corner[:, :, 0], (1, 1), (0, 1))
    south_east = jnp.roll(records_corner[:, :, 2], (-1, 1), (0, 1))
    north_west = jnp.roll(records_corner[:, :, 1], (1, -1), (0, 1))
    north_east = jnp.roll(records_corner[:, :, 3], (-1, -1), (0, 1))
    arrivals = jnp.concatenate([from_west, from_east, from_south, from_north, south_west, south_east, north_west, north_east], 3)
    arrival_particle_records = arrivals[:, :, :5].transpose(2, 0, 1, 3).reshape(5, N_GX, N_GY * NARR)
    arrival_box_index = arrivals[:, :, 5].astype(jnp.int32).reshape(N_GX, N_GY * NARR)
    return (resulting_moisture_ratio, resulting_kelvin_value, resulting_droplet_size, resulting_weighting_factor, arrival_particle_records, arrival_box_index)
```

```python
import functools

import jax
import jax.numpy as jnp
from jax import lax
from jax.experimental import pallas as pl
from jax.experimental.pallas import tpu as pltpu
from jax.sharding import PartitionSpec as P

NEWTON = 4
MIX_HORIZONTAL = 0.2
MIX_VERTICAL = 0.05
EXCESS_FACTOR = 4.2222
CURVATURE = 0.0012
KAPPA_SOLUTE = 0.6
GROWTH_STEP = 200.0
COLLIDE_RATE = 4e-07
VAPOUR_PER_SOURCE = 0.001
WARMING_FACTOR = 0.00249

MESH = pl.DeviceIdType.MESH
DIRS = ((1, 0), (-1, 0), (1, 1), (1, -1), (-1, 1), (-1, -1), (0, 1), (0, -1))
SLOT = {d: n for n, d in enumerate(DIRS)}
SHIFTS = (-1, 0, 1)


def div(x, n):
    return lax.shift_right_arithmetic(x, jnp.int32(n.bit_length() - 1))


def mod(x, n):
    return lax.bitwise_and(x, jnp.int32(n - 1))


def iota(shape, dim):
    return lax.broadcasted_iota(jnp.int32, shape, dim)


def kernel_weights(offset):
    return {
        -1: jnp.maximum(0.5 - offset, 0.0),
        0: 1.0 - jnp.abs(offset - 0.5),
        1: jnp.maximum(offset - 0.5, 0.0),
    }


def pieces(x):
    high = x.astype(jnp.bfloat16)
    rest = x - high.astype(jnp.float32)
    middle = rest.astype(jnp.bfloat16)
    low = (rest - middle.astype(jnp.float32)).astype(jnp.bfloat16)
    return high, middle, low


def pick(tables, hot_row, hot_lane):
    rows = tables[0].shape[0]
    split = [pieces(t) for t in tables]
    stacked = jnp.concatenate([s[n] for n in range(3) for s in split], 0)
    got = jnp.dot(stacked, hot_lane, preferred_element_type=jnp.float32)
    third = rows * len(tables)
    got = (got[:third] + got[third : 2 * third]) + got[2 * third :]
    return [
        jnp.sum(jnp.where(hot_row, got[n * rows : (n + 1) * rows], 0.0), 0, keepdims=True)
        for n in range(len(tables))
    ]


def body(
    sizes,
    moist_in, warm_in, size_in, mult_in, dry_in, east_in, north_in, perm_in,
    lx_in, ly_in, lc_in,
    moist_out, warm_out, size_out, mult_out, rec_out, box_out,
    state, drops, perm, lx, ly, lc,
    pack, halo_row, halo_y, dep_out, dep_in,
    rec, recb, edge, edge_in, edge_rec, edge_box,
    mask, new_size, coal, new_mult, final,
    in_sem, out_sem,
    row_send, row_recv, y_send, y_recv, dep_send, dep_recv,
    rec_send, rec_recv, edge_send, edge_recv,
):
    levels, cx, cy, sd, kx, ky, kc, nx, ny = sizes
    me_x = lax.axis_index("gx")
    me_y = lax.axis_index("gy")

    def at(d):
        return (lax.rem(me_x + d[0] + nx, nx), lax.rem(me_y + d[1] + ny, ny))

    barrier = pltpu.get_barrier_semaphore()
    for d in DIRS:
        pl.semaphore_signal(barrier, inc=1, device_id=at(d), device_id_type=MESH)

    loads = []

    def load(source, target):
        copy = pltpu.make_async_copy(source, target, in_sem.at[len(loads)])
        copy.start()
        loads.append(copy)

    load(moist_in, state.at[0])
    load(warm_in, state.at[1])
    load(lx_in.at[0], lx)
    load(ly_in.at[0], ly)
    load(lc_in.at[0], lc)
    for n, source in enumerate((size_in, mult_in, dry_in, east_in, north_in)):
        load(source, drops.at[n])
    load(perm_in, perm)

    loads[0].wait()
    loads[1].wait()
    for f in range(2):
        for l in range(levels):
            q = 2 * (f * levels + l)
            pack[0, q : q + 2, :] = state[f, l, cx - 2 : cx, :]
            pack[1, q : q + 2, :] = state[f, l, 0:2, :]

    pl.semaphore_wait(barrier, len(DIRS))

    sends = []

    def send(source, target, s_sem, r_sem, d):
        copy = pltpu.make_async_remote_copy(
            src_ref=source, dst_ref=target, send_sem=s_sem, recv_sem=r_sem,
            device_id=at(d), device_id_type=MESH,
        )
        copy.start()
        sends.append(copy)
        return copy

    halo = []
    for n in range(6):
        d = DIRS[n]
        halo.append(
            send(pack.at[0 if d[0] > 0 else 1], halo_row.at[n], row_send.at[n], row_recv.at[n], d)
        )
    for n in range(2):
        for f, source in enumerate((moist_in, warm_in)):
            halo.append(
                send(source, halo_y.at[n, f], y_send.at[n, f], y_recv.at[n, f], DIRS[6 + n])
            )

    for copy in loads[2:]:
        copy.wait()
    rows = sd * levels
    block = cx * cy
    hots = []
    mask[...] = jnp.zeros_like(mask)
    for r, (side, dx) in enumerate(((cx - 1, 1), (0, -1))):
        slots = lx[r : r + 1, :]
        j = mod(slots, cy)
        row = div(slots, block)
        hot_row = iota((rows, kx), 0) == row
        hot_lane = jnp.where(iota((cy, kx), 0) == j, 1.0, 0.0).astype(jnp.bfloat16)
        hots.append((hot_row, hot_lane))
        named = lax.dot_general(
            jnp.where(hot_row, 1.0, 0.0).astype(jnp.bfloat16), hot_lane,
            (((1,), (1,)), ((), ())), preferred_element_type=jnp.float32,
        )
        mask[pl.ds(side, rows, stride=cx), :] = named
        static = pick([drops[n, pl.ds(side, rows, stride=cx), :] for n in (2, 3, 4)], hot_row, hot_lane)
        for n in range(3):
            rec[r, 2 + n, :, :] = static[n]
        target = (mod(row, levels) * cx + mod(mod(div(slots, cy), cx) + dx, cx)) * cy + j
        recb[r, :, :] = jnp.where(slots >= 0, target, -1)
        lanes = pl.ds(r * kx, kx)
        send(rec.at[r, 2:5], rec_out.at[2:5, :, lanes], rec_send.at[r, 0], rec_recv.at[r, 0], (dx, 0))
        send(recb.at[r], box_out.at[:, lanes], rec_send.at[r, 1], rec_recv.at[r, 1], (dx, 0))

    width = 2 * ky + 4 * kc
    slots = jnp.concatenate(
        [ly[0:1, :], ly[1:2, :], lc[0:1, :], lc[2:3, :], lc[1:2, :], lc[3:4, :]], 1
    )
    lane_e = iota((1, width), 1)
    high = (lane_e < ky) | ((lane_e >= 2 * ky) & (lane_e < 2 * ky + 2 * kc))
    move_y = jnp.where(high, 1, -1)
    corner = div(lane_e - 2 * ky, kc)
    move_x = jnp.where(lane_e < 2 * ky, 0, jnp.where(mod(corner, 2) == 0, 1, -1))
    target = (
        mod(div(slots, block), levels) * cx + mod(mod(div(slots, cy), cx) + move_x, cx)
    ) * cy + mod(mod(slots, cy) + move_y, cy)
    edge[5:6, :] = jnp.where(slots >= 0, target, -1).astype(jnp.float32)
    named_e = iota((rows * cx, width), 0) == div(slots, cy)
    high_all = jnp.broadcast_to(high, (rows * cx, width))

    def pick_edge(table):
        both = jnp.where(high_all, table[:, cy - 1 : cy], table[:, 0:1])
        return jnp.sum(jnp.where(named_e, both, 0.0), 0, keepdims=True)

    for n in (2, 3, 4):
        edge[n : n + 1, :] = pick_edge(drops[n])
    edge[6:8, :] = jnp.zeros((2, width), jnp.float32)
    hot_e = jnp.where(named_e, 1.0, 0.0)
    left_high = jnp.max(jnp.where(high_all, hot_e, 0.0), 1, keepdims=True)
    left_low = jnp.max(jnp.where(high_all, 0.0, hot_e), 1, keepdims=True)
    lane_all = iota((rows * cx, cy), 1)
    mask[...] = mask[...] + jnp.where(
        lane_all == cy - 1, left_high, jnp.where(lane_all == 0, left_low, 0.0)
    )

    for copy in halo:
        copy.wait_recv()
    wide = []
    for f in range(2):
        wide.append([])
        for l in range(levels):
            q = 2 * (f * levels + l)
            columns = []
            for c in SHIFTS:
                up = pltpu.roll(halo_row[SLOT[(1, -c)]], (cx - 2 - q) % 8, 0)
                down = pltpu.roll(halo_row[SLOT[(-1, -c)]], (8 - q) % 8, 0)
                centre = state[f, l] if c == 0 else halo_y[SLOT[(0, -c)] - 6, f, l]
                columns.append(jnp.concatenate([up, centre, down], 0))
            wide[f].append(jnp.concatenate(columns, 1))
    mixed = []
    for f in range(2):
        mixed.append([])
        for l in range(levels):
            centre = wide[f][l]
            horizontal = (
                pltpu.roll(centre, 3 * cx - 1, 0) + pltpu.roll(centre, 1, 0)
                + pltpu.roll(centre, 3 * cy - 1, 1) + pltpu.roll(centre, 1, 1)
                - 4.0 * centre
            )
            vertical = wide[f][min(l + 1, levels - 1)] + wide[f][max(l - 1, 0)] - 2.0 * centre
            mixed[f].append(centre + MIX_HORIZONTAL * horizontal + MIX_VERTICAL * vertical)
    window = {(a, b): [] for a in SHIFTS for b in SHIFTS}
    for l in range(levels):
        vapour, warmth = mixed[0][l], mixed[1][l]
        humid = vapour / (
            EXCESS_FACTOR * jnp.exp(17.27 * (warmth - 273.15) / (warmth - 35.86))
        ) - 1.0
        for b in SHIFTS:
            column = humid if b == 0 else pltpu.roll(humid, -b % (3 * cy), 1)
            column = column[:, cy : 2 * cy]
            for a in SHIFTS:
                shifted = column if a == 0 else pltpu.roll(column, -a % (3 * cx), 0)
                window[a, b].append(shifted[cx : 2 * cx])
        final[0, l] = vapour[cx : 2 * cx, cy : 2 * cy]
        final[1, l] = warmth[cx : 2 * cx, cy : 2 * cy]
    window = {key: jnp.concatenate(parts, 0) for key, parts in window.items()}

    grown = []
    mult = []
    deposit = {}
    tall = levels * cx
    for k in range(sd):
        part = pl.ds(k * tall, tall)
        radius, weight, dry = drops[0, part, :], drops[1, part, :], drops[2, part, :]
        wx = kernel_weights(drops[3, part, :])
        wy = kernel_weights(drops[4, part, :])
        forcing = -CURVATURE / radius
        for a in SHIFTS:
            across = sum(wy[b] * window[a, b] for b in SHIFTS)
            forcing = forcing + wx[a] * across
        initial = radius * radius
        lowest = dry * dry
        solute = KAPPA_SOLUTE * lowest * dry
        wetted = initial
        for sweep in range(NEWTON):
            inverse_root = lax.rsqrt(wetted)
            inverse_square = inverse_root * inverse_root
            pull = solute * (inverse_square * inverse_root)
            residue = wetted - initial - GROWTH_STEP * (forcing + pull)
            slope = 1.0 + (1.5 * GROWTH_STEP) * pull * inverse_square
            wetted = jnp.maximum(wetted - residue / slope, lowest)
        root = jnp.sqrt(wetted)
        condensed = weight * (wetted * root - initial * radius)
        for a in SHIFTS:
            along = wx[a] * condensed
            for b in SHIFTS:
                term = wy[b] * along
                deposit[a, b] = term if k == 0 else deposit[a, b] + term
        grown.append(root)
        mult.append(weight)

    lane = iota((cx, cy), 1)
    line = iota((cx, cy), 0)

    def spread(parts, size, dim, index):
        back = pltpu.roll(parts[-1], size - 1, dim)
        ahead = pltpu.roll(parts[1], 1, dim)
        inner = parts[0] + jnp.where(index == size - 1, 0.0, back) + jnp.where(index == 0, 0.0, ahead)
        outer = jnp.where(index == size - 1, back, jnp.where(index == 0, ahead, 0.0))
        return inner, outer

    own = []
    for l in range(levels):
        inner, outer = {}, {}
        for a in SHIFTS:
            parts = {b: deposit[a, b][l * cx : (l + 1) * cx] for b in SHIFTS}
            inner[a], outer[a] = spread(parts, cy, 1, lane)
        kept, to_x = spread(inner, cx, 0, line)
        to_y, to_corner = spread(outer, cx, 0, line)
        own.append(kept)
        dep_out[0, l] = to_x
        dep_out[1, l] = to_corner
        dep_out[2, l] = to_y
    deposits = []
    for n, d in enumerate(DIRS):
        kind = 0 if n < 2 else 1 if n < 6 else 2
        deposits.append(send(dep_out.at[kind], dep_in.at[n], dep_send.at[n], dep_recv.at[n], d))

    order = [perm[k * tall : (k + 1) * tall, :] for k in range(sd)]
    hit = [[order[p] == m for m in range(sd)] for p in range(sd)]

    def member(values, p):
        got = values[0]
        for m in range(1, sd):
            got = jnp.where(hit[p][m], values[m], got)
        return got

    after_radius = []
    after_mult = []
    for pair in range(sd // 2):
        p, q = 2 * pair, 2 * pair + 1
        r_p, r_q = member(grown, p), member(grown, q)
        m_p, m_q = member(mult, p), member(mult, q)
        big = m_p >= m_q
        r_hi, r_lo = jnp.where(big, r_p, r_q), jnp.where(big, r_q, r_p)
        m_hi, m_lo = jnp.where(big, m_p, m_q), jnp.where(big, m_q, m_p)
        total = r_p + r_q
        rate = COLLIDE_RATE * m_hi * total * total * jnp.abs(r_p * r_p - r_q * r_q)
        chance = 1.0 - jnp.exp(-rate)
        volume = r_lo * r_lo * r_lo + chance * r_hi * r_hi * r_hi
        merged = jnp.exp(jnp.log(volume) * (1.0 / 3.0))
        reduced = m_hi - chance * m_lo
        after_radius += [jnp.where(big, r_hi, merged), jnp.where(big, merged, r_hi)]
        after_mult += [jnp.where(big, reduced, m_lo), jnp.where(big, m_lo, reduced)]
    for m in range(sd):
        part = pl.ds(m * tall, tall)
        radius, weight = after_radius[0], after_mult[0]
        for p in range(1, sd):
            radius = jnp.where(hit[p][m], after_radius[p], radius)
            weight = jnp.where(hit[p][m], after_mult[p], weight)
        new_size[part, :] = radius
        coal[part, :] = weight
        new_mult[part, :] = jnp.where(mask[part, :] > 0.0, 0.0, weight)

    stores = []

    def store(source, target):
        copy = pltpu.make_async_copy(source, target, out_sem.at[len(stores)])
        copy.start()
        stores.append(copy)

    store(new_size, size_out)
    store(new_mult, mult_out)

    for r, (side, dx) in enumerate(((cx - 1, 1), (0, -1))):
        late = pick([ref[pl.ds(side, rows, stride=cx), :] for ref in (new_size, coal)], *hots[r])
        for n in range(2):
            rec[r, n, :, :] = late[n]
        lanes = pl.ds(r * kx, kx)
        send(rec.at[r, 0:2], rec_out.at[0:2, :, lanes], rec_send.at[r, 2], rec_recv.at[r, 2], (dx, 0))
    edge[0:1, :] = pick_edge(new_size[...])
    edge[1:2, :] = pick_edge(coal[...])
    edges = []
    for n in range(2, 8):
        edges.append(send(edge, edge_in.at[n - 2], edge_send.at[n - 2], edge_recv.at[n - 2], DIRS[n]))

    for copy in deposits:
        copy.wait_recv()
    for l in range(levels):
        total = own[l]
        for n, (dx, dy) in enumerate(DIRS):
            chosen = None
            if dx:
                chosen = line == (0 if dx > 0 else cx - 1)
            if dy:
                there = lane == (0 if dy > 0 else cy - 1)
                chosen = there if chosen is None else chosen & there
            total = total + jnp.where(chosen, dep_in[n, l], 0.0)
        final[0, l] = final[0, l] - VAPOUR_PER_SOURCE * total
        final[1, l] = final[1, l] + WARMING_FACTOR * total
    store(final.at[0], moist_out)
    store(final.at[1], warm_out)

    for copy in edges:
        copy.wait_recv()
    lane_e = iota((8, width), 1)
    came = edge_in[SLOT[(0, 1)] - 2]
    start = ky
    for d, length in (((0, -1), ky), ((1, 1), kc), ((-1, 1), kc), ((1, -1), kc), ((-1, -1), kc)):
        came = jnp.where(lane_e >= start, edge_in[SLOT[d] - 2], came)
        start += length
    for n in range(5):
        edge_rec[n, :, :] = came[n : n + 1, :]
    edge_box[...] = came[5:6, :].astype(jnp.int32)
    store(edge_rec, rec_out.at[:, :, pl.ds(2 * kx, width)])
    store(edge_box, box_out.at[:, pl.ds(2 * kx, width)])

    halo_and_edges = halo + deposits + edges
    for copy in sends:
        if not any(copy is other for other in halo_and_edges):
            copy.wait_recv()
    for copy in sends:
        copy.wait_send()
    for copy in stores:
        copy.wait()


def per_device(nx, ny, moist, warm, size, mult, dry, east, north, perm, lx, ly, lc):
    levels, cx, cy = moist.shape
    sd = size.shape[0]
    kx, ky, kc = lx.shape[2], ly.shape[2], lc.shape[2]
    narr = 2 * kx + 2 * ky + 4 * kc
    width = 2 * ky + 4 * kc
    slots = sd * levels * cx
    flat = [x.reshape(slots, cy) for x in (size, mult, dry, east, north, perm)]
    f32, i32 = jnp.float32, jnp.int32
    any_space = pl.BlockSpec(memory_space=pl.ANY)
    dma = pltpu.SemaphoreType.DMA
    outs = pl.pallas_call(
        functools.partial(body, (levels, cx, cy, sd, kx, ky, kc, nx, ny)),
        out_shape=(
            jax.ShapeDtypeStruct((levels, cx, cy), f32),
            jax.ShapeDtypeStruct((levels, cx, cy), f32),
            jax.ShapeDtypeStruct((slots, cy), f32),
            jax.ShapeDtypeStruct((slots, cy), f32),
            jax.ShapeDtypeStruct((5, 1, narr), f32),
            jax.ShapeDtypeStruct((1, narr), i32),
        ),
        in_specs=[any_space] * 11,
        out_specs=[any_space] * 6,
        scratch_shapes=[
            pltpu.VMEM((2, levels, cx, cy), f32),
            pltpu.VMEM((5, slots, cy), f32),
            pltpu.VMEM((slots, cy), i32),
            pltpu.VMEM((2, kx), i32),
            pltpu.VMEM((2, ky), i32),
            pltpu.VMEM((4, kc), i32),
            pltpu.VMEM((2, 4 * levels, cy), f32),
            pltpu.VMEM((6, 4 * levels, cy), f32),
            pltpu.VMEM((2, 2, levels, cx, cy), f32),
            pltpu.VMEM((3, levels, cx, cy), f32),
            pltpu.VMEM((8, levels, cx, cy), f32),
            pltpu.VMEM((2, 5, 1, kx), f32),
            pltpu.VMEM((2, 1, kx), i32),
            pltpu.VMEM((8, width), f32),
            pltpu.VMEM((6, 8, width), f32),
            pltpu.VMEM((5, 1, width), f32),
            pltpu.VMEM((1, width), i32),
            pltpu.VMEM((slots, cy), f32),
            pltpu.VMEM((slots, cy), f32),
            pltpu.VMEM((slots, cy), f32),
            pltpu.VMEM((slots, cy), f32),
            pltpu.VMEM((2, levels, cx, cy), f32),
            dma((11,)), dma((6,)),
            dma((6,)), dma((6,)), dma((2, 2)), dma((2, 2)), dma((8,)), dma((8,)),
            dma((2, 3)), dma((2, 3)), dma((6,)), dma((6,)),
        ],
        compiler_params=pltpu.CompilerParams(collective_id=0, has_side_effects=True),
    )(moist, warm, *flat, lx, ly, lc)
    return (
        outs[0], outs[1], outs[2].reshape(size.shape), outs[3].reshape(size.shape), outs[4], outs[5],
    )


def solution(mesh):
    cell, drop, lists = P(None, "gx", "gy"), P(None, None, "gx", "gy"), P("gx", None, "gy")
    return jax.shard_map(
        functools.partial(per_device, mesh.shape["gx"], mesh.shape["gy"]),
        mesh=mesh,
        in_specs=(cell,) * 2 + (drop,) * 6 + (lists,) * 3,
        out_specs=(cell, cell, drop, drop, cell, P("gx", "gy")),
        check_vma=False,
    )
```

```python
import functools

import jax
import jax.numpy as jnp
from jax import lax
from jax.experimental import pallas as pl
from jax.experimental.pallas import tpu as pltpu
from jax.sharding import PartitionSpec as P

NEWTON = 4
MIX_HORIZONTAL = 0.2
MIX_VERTICAL = 0.05
EXCESS_FACTOR = 4.2222
CURVATURE = 0.0012
KAPPA_SOLUTE = 0.6
GROWTH_STEP = 200.0
COLLIDE_RATE = 4e-07
VAPOUR_PER_SOURCE = 0.001
WARMING_FACTOR = 0.00249

MESH = pl.DeviceIdType.MESH
DIRS = ((1, 0), (-1, 0), (1, 1), (1, -1), (-1, 1), (-1, -1), (0, 1), (0, -1))
SLOT = {d: n for n, d in enumerate(DIRS)}
SHIFTS = (-1, 0, 1)


def div(x, n):
    return lax.shift_right_arithmetic(x, jnp.int32(n.bit_length() - 1))


def mod(x, n):
    return lax.bitwise_and(x, jnp.int32(n - 1))


def iota(shape, dim):
    return lax.broadcasted_iota(jnp.int32, shape, dim)


def kernel_weights(offset):
    return {
        -1: jnp.maximum(0.5 - offset, 0.0),
        0: 1.0 - jnp.abs(offset - 0.5),
        1: jnp.maximum(offset - 0.5, 0.0),
    }


def pieces(x):
    high = x.astype(jnp.bfloat16)
    rest = x - high.astype(jnp.float32)
    middle = rest.astype(jnp.bfloat16)
    low = (rest - middle.astype(jnp.float32)).astype(jnp.bfloat16)
    return high, middle, low


def pick(tables, hot_row, hot_lane):
    rows = tables[0].shape[0]
    split = [pieces(t) for t in tables]
    stacked = jnp.concatenate([s[n] for n in range(3) for s in split], 0)
    got = jnp.dot(stacked, hot_lane, preferred_element_type=jnp.float32)
    third = rows * len(tables)
    got = (got[:third] + got[third : 2 * third]) + got[2 * third :]
    return [
        jnp.sum(jnp.where(hot_row, got[n * rows : (n + 1) * rows], 0.0), 0, keepdims=True)
        for n in range(len(tables))
    ]


def body(
    sizes,
    moist_in, warm_in, size_in, mult_in, dry_in, east_in, north_in, perm_in,
    lx_in, ly_in, lc_in,
    moist_out, warm_out, size_out, mult_out, rec_out, box_out,
    state, drops, perm, lx, ly, lc,
    pack, halo_row, halo_y, dep_out, dep_in,
    rec, recb, edge, edge_in,
    mask, coal,
    in_sem,
    row_send, row_recv, y_send, y_recv, dep_send, dep_recv,
    rec_send, rec_recv, edge_send, edge_recv,
):
    levels, cx, cy, sd, kx, ky, kc, nx, ny = sizes
    me_x = lax.axis_index("gx")
    me_y = lax.axis_index("gy")

    def at(d):
        return (lax.rem(me_x + d[0] + nx, nx), lax.rem(me_y + d[1] + ny, ny))

    barrier = pltpu.get_barrier_semaphore()
    for d in DIRS:
        pl.semaphore_signal(barrier, inc=1, device_id=at(d), device_id_type=MESH)

    loads = []

    def load(source, target):
        copy = pltpu.make_async_copy(source, target, in_sem.at[len(loads)])
        copy.start()
        loads.append(copy)

    load(moist_in, state.at[0])
    load(warm_in, state.at[1])
    load(lx_in.at[0], lx)
    load(ly_in.at[0], ly)
    load(lc_in.at[0], lc)
    for n, source in enumerate((size_in, mult_in, dry_in, east_in, north_in)):
        load(source, drops.at[n])
    load(perm_in, perm)

    loads[0].wait()
    loads[1].wait()
    for f in range(2):
        for l in range(levels):
            q = 2 * (f * levels + l)
            pack[0, q : q + 2, :] = state[f, l, cx - 2 : cx, :]
            pack[1, q : q + 2, :] = state[f, l, 0:2, :]

    pl.semaphore_wait(barrier, len(DIRS))

    sends = []

    def send(source, target, s_sem, r_sem, d):
        copy = pltpu.make_async_remote_copy(
            src_ref=source, dst_ref=target, send_sem=s_sem, recv_sem=r_sem,
            device_id=at(d), device_id_type=MESH,
        )
        copy.start()
        sends.append(copy)
        return copy

    halo = []
    for n in range(6):
        d = DIRS[n]
        halo.append(
            send(pack.at[0 if d[0] > 0 else 1], halo_row.at[n], row_send.at[n], row_recv.at[n], d)
        )
    for n in range(2):
        for f, source in enumerate((moist_in, warm_in)):
            halo.append(
                send(source, halo_y.at[n, f], y_send.at[n, f], y_recv.at[n, f], DIRS[6 + n])
            )

    for copy in loads[2:]:
        copy.wait()
    rows = sd * levels
    block = cx * cy
    hots = []
    mask[...] = jnp.zeros_like(mask)
    for r, (side, dx) in enumerate(((cx - 1, 1), (0, -1))):
        slots = lx[r : r + 1, :]
        j = mod(slots, cy)
        row = div(slots, block)
        hot_row = iota((rows, kx), 0) == row
        hot_lane = jnp.where(iota((cy, kx), 0) == j, 1.0, 0.0).astype(jnp.bfloat16)
        hots.append((hot_row, hot_lane))
        named = lax.dot_general(
            jnp.where(hot_row, 1.0, 0.0).astype(jnp.bfloat16), hot_lane,
            (((1,), (1,)), ((), ())), preferred_element_type=jnp.float32,
        )
        mask[pl.ds(side, rows, stride=cx), :] = named
        static = pick([drops[n, pl.ds(side, rows, stride=cx), :] for n in (2, 3, 4)], hot_row, hot_lane)
        for n in range(3):
            rec[r, 2 + n, :, :] = static[n]
        target = (mod(row, levels) * cx + mod(mod(div(slots, cy), cx) + dx, cx)) * cy + j
        recb[r, :, :] = jnp.where(slots >= 0, target, -1)
        lanes = pl.ds(r * kx, kx)
        send(rec.at[r, 2:5], rec_out.at[2:5, :, lanes], rec_send.at[r, 0], rec_recv.at[r, 0], (dx, 0))
        send(recb.at[r], box_out.at[:, lanes], rec_send.at[r, 1], rec_recv.at[r, 1], (dx, 0))

    width = 2 * ky + 4 * kc
    slots = jnp.concatenate(
        [ly[0:1, :], ly[1:2, :], lc[0:1, :], lc[2:3, :], lc[1:2, :], lc[3:4, :]], 1
    )
    lane_e = iota((1, width), 1)
    high = (lane_e < ky) | ((lane_e >= 2 * ky) & (lane_e < 2 * ky + 2 * kc))
    move_y = jnp.where(high, 1, -1)
    corner = div(lane_e - 2 * ky, kc)
    move_x = jnp.where(lane_e < 2 * ky, 0, jnp.where(mod(corner, 2) == 0, 1, -1))
    target = (
        mod(div(slots, block), levels) * cx + mod(mod(div(slots, cy), cx) + move_x, cx)
    ) * cy + mod(mod(slots, cy) + move_y, cy)
    edge[5:6, :] = jnp.where(slots >= 0, target, -1).astype(jnp.float32)
    named_e = iota((rows * cx, width), 0) == div(slots, cy)
    high_all = jnp.broadcast_to(high, (rows * cx, width))

    def pick_edge(table):
        both = jnp.where(high_all, table[:, cy - 1 : cy], table[:, 0:1])
        return jnp.sum(jnp.where(named_e, both, 0.0), 0, keepdims=True)

    for n in (2, 3, 4):
        edge[n : n + 1, :] = pick_edge(drops[n])
    edge[6:8, :] = jnp.zeros((2, width), jnp.float32)
    hot_e = jnp.where(named_e, 1.0, 0.0)
    left_high = jnp.max(jnp.where(high_all, hot_e, 0.0), 1, keepdims=True)
    left_low = jnp.max(jnp.where(high_all, 0.0, hot_e), 1, keepdims=True)
    lane_all = iota((rows * cx, cy), 1)
    mask[...] = mask[...] + jnp.where(
        lane_all == cy - 1, left_high, jnp.where(lane_all == 0, left_low, 0.0)
    )

    for copy in halo:
        copy.wait_recv()
    wide = []
    for f in range(2):
        wide.append([])
        for l in range(levels):
            q = 2 * (f * levels + l)
            columns = []
            for c in SHIFTS:
                up = pltpu.roll(halo_row[SLOT[(1, -c)]], (cx - 2 - q) % 8, 0)
                down = pltpu.roll(halo_row[SLOT[(-1, -c)]], (8 - q) % 8, 0)
                centre = state[f, l] if c == 0 else halo_y[SLOT[(0, -c)] - 6, f, l]
                columns.append(jnp.concatenate([up, centre, down], 0))
            wide[f].append(jnp.concatenate(columns, 1))
    mixed = []
    for f in range(2):
        mixed.append([])
        for l in range(levels):
            centre = wide[f][l]
            horizontal = (
                pltpu.roll(centre, 3 * cx - 1, 0) + pltpu.roll(centre, 1, 0)
                + pltpu.roll(centre, 3 * cy - 1, 1) + pltpu.roll(centre, 1, 1)
                - 4.0 * centre
            )
            vertical = wide[f][min(l + 1, levels - 1)] + wide[f][max(l - 1, 0)] - 2.0 * centre
            mixed[f].append(centre + MIX_HORIZONTAL * horizontal + MIX_VERTICAL * vertical)
    window = {(a, b): [] for a in SHIFTS for b in SHIFTS}
    for l in range(levels):
        vapour, warmth = mixed[0][l], mixed[1][l]
        humid = vapour / (
            EXCESS_FACTOR * jnp.exp(17.27 * (warmth - 273.15) / (warmth - 35.86))
        ) - 1.0
        for b in SHIFTS:
            column = humid if b == 0 else pltpu.roll(humid, -b % (3 * cy), 1)
            column = column[:, cy : 2 * cy]
            for a in SHIFTS:
                shifted = column if a == 0 else pltpu.roll(column, -a % (3 * cx), 0)
                window[a, b].append(shifted[cx : 2 * cx])
        moist_out[l] = vapour[cx : 2 * cx, cy : 2 * cy]
        warm_out[l] = warmth[cx : 2 * cx, cy : 2 * cy]
    window = {key: jnp.concatenate(parts, 0) for key, parts in window.items()}

    grown = []
    mult = []
    deposit = {}
    tall = levels * cx
    for k in range(sd):
        part = pl.ds(k * tall, tall)
        radius, weight, dry = drops[0, part, :], drops[1, part, :], drops[2, part, :]
        wx = kernel_weights(drops[3, part, :])
        wy = kernel_weights(drops[4, part, :])
        forcing = -CURVATURE / radius
        for a in SHIFTS:
            across = sum(wy[b] * window[a, b] for b in SHIFTS)
            forcing = forcing + wx[a] * across
        initial = radius * radius
        lowest = dry * dry
        solute = KAPPA_SOLUTE * lowest * dry
        wetted = initial
        for sweep in range(NEWTON):
            inverse_root = lax.rsqrt(wetted)
            inverse_square = inverse_root * inverse_root
            pull = solute * (inverse_square * inverse_root)
            residue = wetted - initial - GROWTH_STEP * (forcing + pull)
            slope = 1.0 + (1.5 * GROWTH_STEP) * pull * inverse_square
            wetted = jnp.maximum(wetted - residue / slope, lowest)
        root = jnp.sqrt(wetted)
        condensed = weight * (wetted * root - initial * radius)
        for a in SHIFTS:
            along = wx[a] * condensed
            for b in SHIFTS:
                term = wy[b] * along
                deposit[a, b] = term if k == 0 else deposit[a, b] + term
        grown.append(root)
        mult.append(weight)

    lane = iota((cx, cy), 1)
    line = iota((cx, cy), 0)

    def spread(parts, size, dim, index):
        back = pltpu.roll(parts[-1], size - 1, dim)
        ahead = pltpu.roll(parts[1], 1, dim)
        inner = parts[0] + jnp.where(index == size - 1, 0.0, back) + jnp.where(index == 0, 0.0, ahead)
        outer = jnp.where(index == size - 1, back, jnp.where(index == 0, ahead, 0.0))
        return inner, outer

    own = []
    for l in range(levels):
        inner, outer = {}, {}
        for a in SHIFTS:
            parts = {b: deposit[a, b][l * cx : (l + 1) * cx] for b in SHIFTS}
            inner[a], outer[a] = spread(parts, cy, 1, lane)
        kept, to_x = spread(inner, cx, 0, line)
        to_y, to_corner = spread(outer, cx, 0, line)
        own.append(kept)
        dep_out[0, l] = to_x
        dep_out[1, l] = to_corner
        dep_out[2, l] = to_y
    deposits = []
    for n, d in enumerate(DIRS):
        kind = 0 if n < 2 else 1 if n < 6 else 2
        deposits.append(send(dep_out.at[kind], dep_in.at[n], dep_send.at[n], dep_recv.at[n], d))

    order = [perm[k * tall : (k + 1) * tall, :] for k in range(sd)]
    hit = [[order[p] == m for m in range(sd)] for p in range(sd)]

    def member(values, p):
        got = values[0]
        for m in range(1, sd):
            got = jnp.where(hit[p][m], values[m], got)
        return got

    after_radius = []
    after_mult = []
    for pair in range(sd // 2):
        p, q = 2 * pair, 2 * pair + 1
        r_p, r_q = member(grown, p), member(grown, q)
        m_p, m_q = member(mult, p), member(mult, q)
        big = m_p >= m_q
        r_hi, r_lo = jnp.where(big, r_p, r_q), jnp.where(big, r_q, r_p)
        m_hi, m_lo = jnp.where(big, m_p, m_q), jnp.where(big, m_q, m_p)
        total = r_p + r_q
        rate = COLLIDE_RATE * m_hi * total * total * jnp.abs(r_p * r_p - r_q * r_q)
        chance = 1.0 - jnp.exp(-rate)
        volume = r_lo * r_lo * r_lo + chance * r_hi * r_hi * r_hi
        merged = jnp.exp(jnp.log(volume) * (1.0 / 3.0))
        reduced = m_hi - chance * m_lo
        after_radius += [jnp.where(big, r_hi, merged), jnp.where(big, merged, r_hi)]
        after_mult += [jnp.where(big, reduced, m_lo), jnp.where(big, m_lo, reduced)]
    for m in range(sd):
        part = pl.ds(m * tall, tall)
        radius, weight = after_radius[0], after_mult[0]
        for p in range(1, sd):
            radius = jnp.where(hit[p][m], after_radius[p], radius)
            weight = jnp.where(hit[p][m], after_mult[p], weight)
        size_out[part, :] = radius
        coal[part, :] = weight
        mult_out[part, :] = jnp.where(mask[part, :] > 0.0, 0.0, weight)

    for r, (side, dx) in enumerate(((cx - 1, 1), (0, -1))):
        late = pick([ref[pl.ds(side, rows, stride=cx), :] for ref in (size_out, coal)], *hots[r])
        for n in range(2):
            rec[r, n, :, :] = late[n]
        lanes = pl.ds(r * kx, kx)
        send(rec.at[r, 0:2], rec_out.at[0:2, :, lanes], rec_send.at[r, 2], rec_recv.at[r, 2], (dx, 0))
    edge[0:1, :] = pick_edge(size_out[...])
    edge[1:2, :] = pick_edge(coal[...])
    edges = []
    for n in range(2, 8):
        edges.append(send(edge, edge_in.at[n - 2], edge_send.at[n - 2], edge_recv.at[n - 2], DIRS[n]))

    for copy in deposits:
        copy.wait_recv()
    for l in range(levels):
        total = own[l]
        for n, (dx, dy) in enumerate(DIRS):
            chosen = None
            if dx:
                chosen = line == (0 if dx > 0 else cx - 1)
            if dy:
                there = lane == (0 if dy > 0 else cy - 1)
                chosen = there if chosen is None else chosen & there
            total = total + jnp.where(chosen, dep_in[n, l], 0.0)
        moist_out[l] = moist_out[l] - VAPOUR_PER_SOURCE * total
        warm_out[l] = warm_out[l] + WARMING_FACTOR * total

    for copy in edges:
        copy.wait_recv()
    lane_e = iota((8, width), 1)
    came = edge_in[SLOT[(0, 1)] - 2]
    start = ky
    for d, length in (((0, -1), ky), ((1, 1), kc), ((-1, 1), kc), ((1, -1), kc), ((-1, -1), kc)):
        came = jnp.where(lane_e >= start, edge_in[SLOT[d] - 2], came)
        start += length
    for n in range(5):
        rec_out[n, :, pl.ds(2 * kx, width)] = came[n : n + 1, :]
    box_out[:, pl.ds(2 * kx, width)] = came[5:6, :].astype(jnp.int32)

    halo_and_edges = halo + deposits + edges
    for copy in sends:
        if not any(copy is other for other in halo_and_edges):
            copy.wait_recv()
    for copy in sends:
        copy.wait_send()


def publish(*refs):
    count = len(refs) // 2
    sems = refs[-1]
    copies = [
        pltpu.make_async_copy(refs[n], refs[count + n], sems.at[n]) for n in range(count)
    ]
    for copy in copies:
        copy.start()
    for copy in copies:
        copy.wait()


def per_device(nx, ny, moist, warm, size, mult, dry, east, north, perm, lx, ly, lc):
    levels, cx, cy = moist.shape
    sd = size.shape[0]
    kx, ky, kc = lx.shape[2], ly.shape[2], lc.shape[2]
    narr = 2 * kx + 2 * ky + 4 * kc
    width = 2 * ky + 4 * kc
    slots = sd * levels * cx
    flat = [x.reshape(slots, cy) for x in (size, mult, dry, east, north, perm)]
    f32, i32 = jnp.float32, jnp.int32
    any_space = pl.BlockSpec(memory_space=pl.ANY)
    vmem_space = pl.BlockSpec(memory_space=pltpu.VMEM)
    dma = pltpu.SemaphoreType.DMA
    shapes = (
        ((levels, cx, cy), f32),
        ((levels, cx, cy), f32),
        ((slots, cy), f32),
        ((slots, cy), f32),
        ((5, 1, narr), f32),
        ((1, narr), i32),
    )
    outs = pl.pallas_call(
        functools.partial(body, (levels, cx, cy, sd, kx, ky, kc, nx, ny)),
        out_shape=tuple(pltpu.VMEM(*s) for s in shapes),
        in_specs=[any_space] * 11,
        out_specs=[vmem_space] * 6,
        scratch_shapes=[
            pltpu.VMEM((2, levels, cx, cy), f32),
            pltpu.VMEM((5, slots, cy), f32),
            pltpu.VMEM((slots, cy), i32),
            pltpu.VMEM((2, kx), i32),
            pltpu.VMEM((2, ky), i32),
            pltpu.VMEM((4, kc), i32),
            pltpu.VMEM((2, 4 * levels, cy), f32),
            pltpu.VMEM((6, 4 * levels, cy), f32),
            pltpu.VMEM((2, 2, levels, cx, cy), f32),
            pltpu.VMEM((3, levels, cx, cy), f32),
            pltpu.VMEM((8, levels, cx, cy), f32),
            pltpu.VMEM((2, 5, 1, kx), f32),
            pltpu.VMEM((2, 1, kx), i32),
            pltpu.VMEM((8, width), f32),
            pltpu.VMEM((6, 8, width), f32),
            pltpu.VMEM((slots, cy), f32),
            pltpu.VMEM((slots, cy), f32),
            dma((11,)),
            dma((6,)), dma((6,)), dma((2, 2)), dma((2, 2)), dma((8,)), dma((8,)),
            dma((2, 3)), dma((2, 3)), dma((6,)), dma((6,)),
        ],
        compiler_params=pltpu.CompilerParams(collective_id=0, has_side_effects=True),
    )(moist, warm, *flat, lx, ly, lc)
    outs = pl.pallas_call(
        publish,
        out_shape=tuple(jax.ShapeDtypeStruct(*s) for s in shapes),
        in_specs=[vmem_space] * 6,
        out_specs=[any_space] * 6,
        scratch_shapes=[dma((6,))],
    )(*[pltpu.with_memory_space_constraint(x, pltpu.VMEM) for x in outs])
    return (
        outs[0], outs[1], outs[2].reshape(size.shape), outs[3].reshape(size.shape), outs[4], outs[5],
    )


def solution(mesh):
    cell, drop, lists = P(None, "gx", "gy"), P(None, None, "gx", "gy"), P("gx", None, "gy")
    return jax.shard_map(
        functools.partial(per_device, mesh.shape["gx"], mesh.shape["gy"]),
        mesh=mesh,
        in_specs=(cell,) * 2 + (drop,) * 6 + (lists,) * 3,
        out_specs=(cell, cell, drop, drop, cell, P("gx", "gy")),
        check_vma=False,
    )
```

```python
import functools

import jax
import jax.numpy as jnp
from jax import lax
from jax.experimental import pallas as pl
from jax.experimental.pallas import tpu as pltpu
from jax.sharding import PartitionSpec as P

NEWTON = 4
MIX_HORIZONTAL = 0.2
MIX_VERTICAL = 0.05
EXCESS_FACTOR = 4.2222
CURVATURE = 0.0012
KAPPA_SOLUTE = 0.6
GROWTH_STEP = 200.0
COLLIDE_RATE = 4e-07
VAPOUR_PER_SOURCE = 0.001
WARMING_FACTOR = 0.00249

MESH = pl.DeviceIdType.MESH
DIRS = ((1, 0), (-1, 0), (1, 1), (1, -1), (-1, 1), (-1, -1), (0, 1), (0, -1))
SLOT = {d: n for n, d in enumerate(DIRS)}
SHIFTS = (-1, 0, 1)


def div(x, n):
    return lax.shift_right_arithmetic(x, jnp.int32(n.bit_length() - 1))


def mod(x, n):
    return lax.bitwise_and(x, jnp.int32(n - 1))


def iota(shape, dim):
    return lax.broadcasted_iota(jnp.int32, shape, dim)


def kernel_weights(offset):
    return {
        -1: jnp.maximum(0.5 - offset, 0.0),
        0: 1.0 - jnp.abs(offset - 0.5),
        1: jnp.maximum(offset - 0.5, 0.0),
    }


def pieces(x):
    high = x.astype(jnp.bfloat16)
    rest = x - high.astype(jnp.float32)
    middle = rest.astype(jnp.bfloat16)
    low = (rest - middle.astype(jnp.float32)).astype(jnp.bfloat16)
    return high, middle, low


def pick(tables, hot_row, hot_lane):
    rows = tables[0].shape[0]
    split = [pieces(t) for t in tables]
    stacked = jnp.concatenate([s[n] for n in range(3) for s in split], 0)
    got = jnp.dot(stacked, hot_lane, preferred_element_type=jnp.float32)
    third = rows * len(tables)
    got = (got[:third] + got[third : 2 * third]) + got[2 * third :]
    return [
        jnp.sum(jnp.where(hot_row, got[n * rows : (n + 1) * rows], 0.0), 0, keepdims=True)
        for n in range(len(tables))
    ]


def body(
    sizes,
    moist_in, warm_in, size_in, mult_in, dry_in, east_in, north_in, perm_in,
    lx_in, ly_in, lc_in,
    moist_out, warm_out, size_out, mult_out, rec_out, box_out,
    state, drops, perm, lx, ly, lc,
    pack, halo_row, halo_y, dep_out, dep_in, dep_rim, rim_in,
    rec, recb, edge, edge_in,
    mask, coal,
    in_sem,
    row_send, row_recv, y_send, y_recv, dep_send, dep_recv,
    rec_send, rec_recv, edge_send, edge_recv,
):
    levels, cx, cy, sd, kx, ky, kc, nx, ny = sizes
    me_x = lax.axis_index("gx")
    me_y = lax.axis_index("gy")

    def at(d):
        return (lax.rem(me_x + d[0] + nx, nx), lax.rem(me_y + d[1] + ny, ny))

    barrier = pltpu.get_barrier_semaphore()
    for d in DIRS:
        pl.semaphore_signal(barrier, inc=1, device_id=at(d), device_id_type=MESH)

    loads = []

    def load(source, target):
        copy = pltpu.make_async_copy(source, target, in_sem.at[len(loads)])
        copy.start()
        loads.append(copy)

    load(moist_in, state.at[0])
    load(warm_in, state.at[1])
    load(lx_in.at[0], lx)
    load(ly_in.at[0], ly)
    load(lc_in.at[0], lc)
    for n, source in enumerate((size_in, mult_in, dry_in, east_in, north_in)):
        load(source, drops.at[n])
    load(perm_in, perm)

    loads[0].wait()
    loads[1].wait()
    for f in range(2):
        for l in range(levels):
            q = 2 * (f * levels + l)
            pack[0, q : q + 2, :] = state[f, l, cx - 2 : cx, :]
            pack[1, q : q + 2, :] = state[f, l, 0:2, :]

    pl.semaphore_wait(barrier, len(DIRS))

    sends = []

    def send(source, target, s_sem, r_sem, d):
        copy = pltpu.make_async_remote_copy(
            src_ref=source, dst_ref=target, send_sem=s_sem, recv_sem=r_sem,
            device_id=at(d), device_id_type=MESH,
        )
        copy.start()
        sends.append(copy)
        return copy

    halo = []
    for n in range(6):
        d = DIRS[n]
        halo.append(
            send(pack.at[0 if d[0] > 0 else 1], halo_row.at[n], row_send.at[n], row_recv.at[n], d)
        )
    for n in range(2):
        for f, source in enumerate((moist_in, warm_in)):
            halo.append(
                send(source, halo_y.at[n, f], y_send.at[n, f], y_recv.at[n, f], DIRS[6 + n])
            )

    for copy in loads[2:]:
        copy.wait()
    rows = sd * levels
    block = cx * cy
    hots = []
    mask[...] = jnp.zeros_like(mask)
    for r, (side, dx) in enumerate(((cx - 1, 1), (0, -1))):
        slots = lx[r : r + 1, :]
        j = mod(slots, cy)
        row = div(slots, block)
        hot_row = iota((rows, kx), 0) == row
        hot_lane = jnp.where(iota((cy, kx), 0) == j, 1.0, 0.0).astype(jnp.bfloat16)
        hots.append((hot_row, hot_lane))
        named = lax.dot_general(
            jnp.where(hot_row, 1.0, 0.0).astype(jnp.bfloat16), hot_lane,
            (((1,), (1,)), ((), ())), preferred_element_type=jnp.float32,
        )
        mask[pl.ds(side, rows, stride=cx), :] = named
        static = pick([drops[n, pl.ds(side, rows, stride=cx), :] for n in (2, 3, 4)], hot_row, hot_lane)
        for n in range(3):
            rec[r, 2 + n, :, :] = static[n]
        target = (mod(row, levels) * cx + mod(mod(div(slots, cy), cx) + dx, cx)) * cy + j
        recb[r, :, :] = jnp.where(slots >= 0, target, -1)
        lanes = pl.ds(r * kx, kx)
        send(rec.at[r, 2:5], rec_out.at[2:5, :, lanes], rec_send.at[r, 0], rec_recv.at[r, 0], (dx, 0))
        send(recb.at[r], box_out.at[:, lanes], rec_send.at[r, 1], rec_recv.at[r, 1], (dx, 0))

    width = 2 * ky + 4 * kc
    slots = jnp.concatenate(
        [ly[0:1, :], ly[1:2, :], lc[0:1, :], lc[2:3, :], lc[1:2, :], lc[3:4, :]], 1
    )
    lane_e = iota((1, width), 1)
    high = (lane_e < ky) | ((lane_e >= 2 * ky) & (lane_e < 2 * ky + 2 * kc))
    move_y = jnp.where(high, 1, -1)
    corner = div(lane_e - 2 * ky, kc)
    move_x = jnp.where(lane_e < 2 * ky, 0, jnp.where(mod(corner, 2) == 0, 1, -1))
    target = (
        mod(div(slots, block), levels) * cx + mod(mod(div(slots, cy), cx) + move_x, cx)
    ) * cy + mod(mod(slots, cy) + move_y, cy)
    edge[5:6, :] = jnp.where(slots >= 0, target, -1).astype(jnp.float32)
    named_e = iota((rows * cx, width), 0) == div(slots, cy)
    high_all = jnp.broadcast_to(high, (rows * cx, width))

    def pick_edge(table):
        both = jnp.where(high_all, table[:, cy - 1 : cy], table[:, 0:1])
        return jnp.sum(jnp.where(named_e, both, 0.0), 0, keepdims=True)

    for n in (2, 3, 4):
        edge[n : n + 1, :] = pick_edge(drops[n])
    edge[6:8, :] = jnp.zeros((2, width), jnp.float32)
    hot_e = jnp.where(named_e, 1.0, 0.0)
    left_high = jnp.max(jnp.where(high_all, hot_e, 0.0), 1, keepdims=True)
    left_low = jnp.max(jnp.where(high_all, 0.0, hot_e), 1, keepdims=True)
    lane_all = iota((rows * cx, cy), 1)
    mask[...] = mask[...] + jnp.where(
        lane_all == cy - 1, left_high, jnp.where(lane_all == 0, left_low, 0.0)
    )

    for copy in halo:
        copy.wait_recv()
    wide = []
    for f in range(2):
        wide.append([])
        for l in range(levels):
            q = 2 * (f * levels + l)
            columns = []
            for c in SHIFTS:
                up = pltpu.roll(halo_row[SLOT[(1, -c)]], (cx - 2 - q) % 8, 0)
                down = pltpu.roll(halo_row[SLOT[(-1, -c)]], (8 - q) % 8, 0)
                centre = state[f, l] if c == 0 else halo_y[SLOT[(0, -c)] - 6, f, l]
                columns.append(jnp.concatenate([up, centre, down], 0))
            wide[f].append(jnp.concatenate(columns, 1))
    mixed = []
    for f in range(2):
        mixed.append([])
        for l in range(levels):
            centre = wide[f][l]
            horizontal = (
                pltpu.roll(centre, 3 * cx - 1, 0) + pltpu.roll(centre, 1, 0)
                + pltpu.roll(centre, 3 * cy - 1, 1) + pltpu.roll(centre, 1, 1)
                - 4.0 * centre
            )
            vertical = wide[f][min(l + 1, levels - 1)] + wide[f][max(l - 1, 0)] - 2.0 * centre
            mixed[f].append(centre + MIX_HORIZONTAL * horizontal + MIX_VERTICAL * vertical)
    window = {(a, b): [] for a in SHIFTS for b in SHIFTS}
    for l in range(levels):
        vapour, warmth = mixed[0][l], mixed[1][l]
        humid = vapour / (
            EXCESS_FACTOR * jnp.exp(17.27 * (warmth - 273.15) / (warmth - 35.86))
        ) - 1.0
        for b in SHIFTS:
            column = humid if b == 0 else pltpu.roll(humid, -b % (3 * cy), 1)
            column = column[:, cy : 2 * cy]
            for a in SHIFTS:
                shifted = column if a == 0 else pltpu.roll(column, -a % (3 * cx), 0)
                window[a, b].append(shifted[cx : 2 * cx])
        moist_out[l] = vapour[cx : 2 * cx, cy : 2 * cy]
        warm_out[l] = warmth[cx : 2 * cx, cy : 2 * cy]
    window = {key: jnp.concatenate(parts, 0) for key, parts in window.items()}

    grown = []
    mult = []
    deposit = {}
    tall = levels * cx
    for k in range(sd):
        part = pl.ds(k * tall, tall)
        radius, weight, dry = drops[0, part, :], drops[1, part, :], drops[2, part, :]
        wx = kernel_weights(drops[3, part, :])
        wy = kernel_weights(drops[4, part, :])
        forcing = -CURVATURE / radius
        for a in SHIFTS:
            across = sum(wy[b] * window[a, b] for b in SHIFTS)
            forcing = forcing + wx[a] * across
        initial = radius * radius
        lowest = dry * dry
        solute = KAPPA_SOLUTE * lowest * dry
        wetted = initial
        for sweep in range(NEWTON):
            inverse_root = lax.rsqrt(wetted)
            inverse_square = inverse_root * inverse_root
            pull = solute * (inverse_square * inverse_root)
            residue = wetted - initial - GROWTH_STEP * (forcing + pull)
            slope = 1.0 + (1.5 * GROWTH_STEP) * pull * inverse_square
            wetted = jnp.maximum(wetted - residue / slope, lowest)
        root = jnp.sqrt(wetted)
        condensed = weight * (wetted * root - initial * radius)
        for a in SHIFTS:
            along = wx[a] * condensed
            for b in SHIFTS:
                term = wy[b] * along
                deposit[a, b] = term if k == 0 else deposit[a, b] + term
        grown.append(root)
        mult.append(weight)

    lane = iota((cx, cy), 1)
    line = iota((cx, cy), 0)

    def spread(parts, size, dim, index):
        back = pltpu.roll(parts[-1], size - 1, dim)
        ahead = pltpu.roll(parts[1], 1, dim)
        inner = parts[0] + jnp.where(index == size - 1, 0.0, back) + jnp.where(index == 0, 0.0, ahead)
        outer = jnp.where(index == size - 1, back, jnp.where(index == 0, ahead, 0.0))
        return inner, outer

    own = []
    packed = jnp.zeros((cx, cy), jnp.float32)
    for l in range(levels):
        inner, outer = {}, {}
        for a in SHIFTS:
            parts = {b: deposit[a, b][l * cx : (l + 1) * cx] for b in SHIFTS}
            inner[a], outer[a] = spread(parts, cy, 1, lane)
        kept, to_x = spread(inner, cx, 0, line)
        to_y, to_corner = spread(outer, cx, 0, line)
        own.append(kept)
        dep_out[l] = to_y
        packed = packed + (pltpu.roll(to_x, 2 * l, 0) if l else to_x) + pltpu.roll(to_corner, 2 * (levels + l), 0)
    dep_rim[...] = packed
    deposits = []
    for n, d in enumerate(DIRS):
        source, target = (dep_rim, rim_in.at[n]) if n < 6 else (dep_out, dep_in.at[n - 6])
        deposits.append(send(source, target, dep_send.at[n], dep_recv.at[n], d))

    order = [perm[k * tall : (k + 1) * tall, :] for k in range(sd)]
    hit = [[order[p] == m for m in range(sd)] for p in range(sd)]

    def member(values, p):
        got = values[0]
        for m in range(1, sd):
            got = jnp.where(hit[p][m], values[m], got)
        return got

    after_radius = []
    after_mult = []
    for pair in range(sd // 2):
        p, q = 2 * pair, 2 * pair + 1
        r_p, r_q = member(grown, p), member(grown, q)
        m_p, m_q = member(mult, p), member(mult, q)
        big = m_p >= m_q
        r_hi, r_lo = jnp.where(big, r_p, r_q), jnp.where(big, r_q, r_p)
        m_hi, m_lo = jnp.where(big, m_p, m_q), jnp.where(big, m_q, m_p)
        total = r_p + r_q
        rate = COLLIDE_RATE * m_hi * total * total * jnp.abs(r_p * r_p - r_q * r_q)
        chance = 1.0 - jnp.exp(-rate)
        volume = r_lo * r_lo * r_lo + chance * r_hi * r_hi * r_hi
        merged = jnp.exp(jnp.log(volume) * (1.0 / 3.0))
        reduced = m_hi - chance * m_lo
        after_radius += [jnp.where(big, r_hi, merged), jnp.where(big, merged, r_hi)]
        after_mult += [jnp.where(big, reduced, m_lo), jnp.where(big, m_lo, reduced)]
    for m in range(sd):
        part = pl.ds(m * tall, tall)
        radius, weight = after_radius[0], after_mult[0]
        for p in range(1, sd):
            radius = jnp.where(hit[p][m], after_radius[p], radius)
            weight = jnp.where(hit[p][m], after_mult[p], weight)
        size_out[part, :] = radius
        coal[part, :] = weight
        mult_out[part, :] = jnp.where(mask[part, :] > 0.0, 0.0, weight)

    for r, (side, dx) in enumerate(((cx - 1, 1), (0, -1))):
        late = pick([ref[pl.ds(side, rows, stride=cx), :] for ref in (size_out, coal)], *hots[r])
        for n in range(2):
            rec[r, n, :, :] = late[n]
        lanes = pl.ds(r * kx, kx)
        send(rec.at[r, 0:2], rec_out.at[0:2, :, lanes], rec_send.at[r, 2], rec_recv.at[r, 2], (dx, 0))
    edge[0:1, :] = pick_edge(size_out[...])
    edge[1:2, :] = pick_edge(coal[...])
    edges = []
    for n in range(2, 8):
        edges.append(send(edge, edge_in.at[n - 2], edge_send.at[n - 2], edge_recv.at[n - 2], DIRS[n]))

    for copy in deposits:
        copy.wait_recv()
    for l in range(levels):
        total = own[l]
        for n, (dx, dy) in enumerate(DIRS):
            chosen = None
            if dx:
                chosen = line == (0 if dx > 0 else cx - 1)
            if dy:
                there = lane == (0 if dy > 0 else cy - 1)
                chosen = there if chosen is None else chosen & there
            if n < 6:
                q = l if n < 2 else levels + l
                came = pltpu.roll(rim_in[n], cx - 2 * q, 0) if q else rim_in[n]
            else:
                came = dep_in[n - 6, l]
            total = total + jnp.where(chosen, came, 0.0)
        moist_out[l] = moist_out[l] - VAPOUR_PER_SOURCE * total
        warm_out[l] = warm_out[l] + WARMING_FACTOR * total

    for copy in edges:
        copy.wait_recv()
    lane_e = iota((8, width), 1)
    came = edge_in[SLOT[(0, 1)] - 2]
    start = ky
    for d, length in (((0, -1), ky), ((1, 1), kc), ((-1, 1), kc), ((1, -1), kc), ((-1, -1), kc)):
        came = jnp.where(lane_e >= start, edge_in[SLOT[d] - 2], came)
        start += length
    for n in range(5):
        rec_out[n, :, pl.ds(2 * kx, width)] = came[n : n + 1, :]
    box_out[:, pl.ds(2 * kx, width)] = came[5:6, :].astype(jnp.int32)

    halo_and_edges = halo + deposits + edges
    for copy in sends:
        if not any(copy is other for other in halo_and_edges):
            copy.wait_recv()
    for copy in sends:
        copy.wait_send()


def publish(*refs):
    count = len(refs) // 2
    sems = refs[-1]
    copies = [
        pltpu.make_async_copy(refs[n], refs[count + n], sems.at[n]) for n in range(count)
    ]
    for copy in copies:
        copy.start()
    for copy in copies:
        copy.wait()


def per_device(nx, ny, moist, warm, size, mult, dry, east, north, perm, lx, ly, lc):
    levels, cx, cy = moist.shape
    sd = size.shape[0]
    kx, ky, kc = lx.shape[2], ly.shape[2], lc.shape[2]
    narr = 2 * kx + 2 * ky + 4 * kc
    width = 2 * ky + 4 * kc
    slots = sd * levels * cx
    flat = [x.reshape(slots, cy) for x in (size, mult, dry, east, north, perm)]
    f32, i32 = jnp.float32, jnp.int32
    any_space = pl.BlockSpec(memory_space=pl.ANY)
    vmem_space = pl.BlockSpec(memory_space=pltpu.VMEM)
    dma = pltpu.SemaphoreType.DMA
    shapes = (
        ((levels, cx, cy), f32),
        ((levels, cx, cy), f32),
        ((slots, cy), f32),
        ((slots, cy), f32),
        ((5, 1, narr), f32),
        ((1, narr), i32),
    )
    outs = pl.pallas_call(
        functools.partial(body, (levels, cx, cy, sd, kx, ky, kc, nx, ny)),
        out_shape=tuple(pltpu.VMEM(*s) for s in shapes),
        in_specs=[any_space] * 11,
        out_specs=[vmem_space] * 6,
        scratch_shapes=[
            pltpu.VMEM((2, levels, cx, cy), f32),
            pltpu.VMEM((5, slots, cy), f32),
            pltpu.VMEM((slots, cy), i32),
            pltpu.VMEM((2, kx), i32),
            pltpu.VMEM((2, ky), i32),
            pltpu.VMEM((4, kc), i32),
            pltpu.VMEM((2, 4 * levels, cy), f32),
            pltpu.VMEM((6, 4 * levels, cy), f32),
            pltpu.VMEM((2, 2, levels, cx, cy), f32),
            pltpu.VMEM((levels, cx, cy), f32),
            pltpu.VMEM((2, levels, cx, cy), f32),
            pltpu.VMEM((cx, cy), f32),
            pltpu.VMEM((6, cx, cy), f32),
            pltpu.VMEM((2, 5, 1, kx), f32),
            pltpu.VMEM((2, 1, kx), i32),
            pltpu.VMEM((8, width), f32),
            pltpu.VMEM((6, 8, width), f32),
            pltpu.VMEM((slots, cy), f32),
            pltpu.VMEM((slots, cy), f32),
            dma((11,)),
            dma((6,)), dma((6,)), dma((2, 2)), dma((2, 2)), dma((8,)), dma((8,)),
            dma((2, 3)), dma((2, 3)), dma((6,)), dma((6,)),
        ],
        compiler_params=pltpu.CompilerParams(collective_id=0, has_side_effects=True),
    )(moist, warm, *flat, lx, ly, lc)
    outs = pl.pallas_call(
        publish,
        out_shape=tuple(jax.ShapeDtypeStruct(*s) for s in shapes),
        in_specs=[vmem_space] * 6,
        out_specs=[any_space] * 6,
        scratch_shapes=[dma((6,))],
    )(*[pltpu.with_memory_space_constraint(x, pltpu.VMEM) for x in outs])
    return (
        outs[0], outs[1], outs[2].reshape(size.shape), outs[3].reshape(size.shape), outs[4], outs[5],
    )


def solution(mesh):
    cell, drop, lists = P(None, "gx", "gy"), P(None, None, "gx", "gy"), P("gx", None, "gy")
    return jax.shard_map(
        functools.partial(per_device, mesh.shape["gx"], mesh.shape["gy"]),
        mesh=mesh,
        in_specs=(cell,) * 2 + (drop,) * 6 + (lists,) * 3,
        out_specs=(cell, cell, drop, drop, cell, P("gx", "gy")),
        check_vma=False,
    )
```
